512 devices in a mesh: ctx: 8 (over x_hi, y), fsdp: 64 (over x_lo, z, core).
Axes of the slice: x: 4 (x_hi: 2, x_lo: 2; x = x_hi * 2 + x_lo), y: 4, z: 16, core: 2. Of those that a mesh axis runs over, the one named last changes fastest.
Arguments:
- hidden_rows: bfloat16 [64, 1024, 4608], P('fsdp', 'ctx'), may hold values from -6 to 6
- query_proj: bfloat16 [64, 1024, 2048], P('fsdp', 'ctx'), may hold values from -10 to 10
- key_proj: bfloat16 [64, 1024, 1024], P('fsdp', 'ctx'), may hold values from -10 to 10
- value_proj: bfloat16 [64, 1024, 1024], P('fsdp', 'ctx'), may hold values from -6 to 6
- order_pos: int32 [64, 1024], P('fsdp', 'ctx'), may hold values from 0 to 1023, each once within a row
- post_gain: float32 [4608], replicated, may hold values from 0.5 to 1.5
- out_weight: bfloat16 [2048, 4608], P('fsdp', 'ctx'), may hold values from -0.125 to 0.125
Outputs:
- residual_out: bfloat16 [64, 1024, 4608], P('fsdp', 'ctx')
The draws below stay inside these ranges and needn't reach their ends.
Inputs may be any that keep to these rules, and one draw needn't show every extreme that they name: Each document's row of order_pos holds every position of 0 to 1023 exactly once.
All inputs are finite; a program needn't handle non-finite values.
Results may differ from the reference program's by a relative error of at most 0.0053.
Values may be sent and summed in bfloat16 or wider, within the bound.
A program may use at most 64 MiB of HBM per device.

```python
import jax
import jax.numpy as jnp
from jax import lax

D = 4608
HQ = 16
HK = 8
DH = 128
LENGTH = 1024
DOCS = 64


def steps_of(stream_key, shape, pieces, smallest, largest):
    loudness, own = 1.0, jax.random.fold_in(stream_key, 6)
    for axis_at, shards_of in pieces:
        heights = jnp.exp(jax.random.uniform(jax.random.fold_in(own, axis_at), (shards_of,), jnp.float32, smallest / len(pieces), largest / len(pieces)))
        loudness = loudness * jnp.repeat(heights, shape[axis_at] // shards_of).reshape([-1 if axis == axis_at else 1 for axis in range(len(shape))])
    return loudness


def centred(stream_key, dims, scale, most, split=(), dtype=jnp.bfloat16):
    array = scale * jax.random.normal(stream_key, dims, jnp.float32)
    if split:
        array = array * steps_of(stream_key, dims, split, -0.22, 0.18)
    return jnp.clip(array, -most, most).astype(dtype)


def setup_inputs(seed: int = 0) -> dict:
    streams_of = jax.random.split(jax.random.key(seed), 8)
    return {
        "hidden_rows": centred(streams_of[0], (DOCS, LENGTH, D), 1.0, 6.0, ((0, 64), (1, 8))),
        "query_proj": centred(streams_of[1], (DOCS, LENGTH, HQ * DH), 1.7, 10.0, ((0, 64), (1, 8))),
        "key_proj": centred(streams_of[2], (DOCS, LENGTH, HK * DH), 1.7, 10.0, ((0, 64), (1, 8))),
        "value_proj": centred(streams_of[3], (DOCS, LENGTH, HK * DH), 1.0, 6.0, ((0, 64), (1, 8))),
        "order_pos": jax.vmap(lambda own: jax.random.permutation(own, LENGTH))(jax.random.split(streams_of[4], DOCS)).reshape((DOCS, LENGTH)).astype(jnp.int32),
        "post_gain": jnp.clip(1.0 + 0.1 * jax.random.normal(streams_of[5], (D,), jnp.float32), 0.5, 1.5),
        "out_weight": centred(streams_of[6], (HQ * DH, D), (HQ * DH) ** -0.5, 0.125, ((0, 64), (1, 8))),
    }


score_scale = 1.0 / 12.0
soft_cap = 50.0
norm_eps = 1e-06

def reference(hidden_rows, query_proj, key_proj, value_proj, order_pos, post_gain, out_weight):
    groups = HQ // HK

    def score_document(operands):
        hidden_doc, query_rows, key_rows, value_rows, position = operands
        query_heads = query_rows.astype(jnp.float32).reshape(LENGTH, HK, groups, DH)
        key_heads = key_rows.astype(jnp.float32).reshape(LENGTH, HK, DH)
        value_heads = value_rows.astype(jnp.float32).reshape(LENGTH, HK, DH)
        scores = jnp.einsum('thgd,nhd->hgtn', query_heads, key_heads) * score_scale
        capped = soft_cap * jnp.tanh(scores / soft_cap)
        visible = position[None, :] <= position[:, None]
        weights = jnp.where(visible, jnp.exp(capped), jnp.float32(0.0))
        rounded = lax.optimization_barrier(weights.astype(jnp.bfloat16)).astype(jnp.float32)
        numerator = jnp.einsum('hgtn,nhd->thgd', rounded, value_heads)
        denominator = jnp.transpose(lax.optimization_barrier(jnp.sum(weights, axis=-1)), (2, 0, 1))
        attended = (numerator / denominator[..., None]).astype(jnp.bfloat16).reshape(LENGTH, HQ * DH)
        projected = jnp.dot(attended, out_weight, preferred_element_type=jnp.float32).astype(jnp.bfloat16)
        widened = projected.astype(jnp.float32)
        normed = widened * lax.rsqrt(lax.optimization_barrier(jnp.mean(widened * widened, axis=-1, keepdims=True)) + norm_eps) * post_gain
        return (hidden_doc.astype(jnp.float32) + normed).astype(jnp.bfloat16)
    return lax.map(score_document, (hidden_rows, query_proj, key_proj, value_proj, order_pos))
```

```python
import jax
import jax.numpy as jnp
from jax import lax
from jax.experimental import pallas as pl
from jax.experimental.pallas import tpu as pltpu
from jax.sharding import PartitionSpec as P

D = 4608
TB = 128
CB = 576
NZ = 16
INNER = 1.0 / 600.0
OUTER = 50.0 * 1.4426950408889634
NORM_EPS = 1e-06
MESH = pl.DeviceIdType.MESH


def body(
    hid, q, k, v, pos, gain, w, out,
    qbuf, kbuf, vbuf, pbuf, bias, att, wg, acc, obuf, rows, hbuf,
    loc, q_s, q_r, k_s, k_r, v_s, v_r, p_s, p_r, wx_s, wx_r,
    rg_s, rg_r, sb_s, sb_r, a_s, a_r, f_s, f_r, o_s, o_r,
):
    ctx = lax.axis_index("ctx")
    fs = lax.axis_index("fsdp")
    xh, y = ctx // 4, ctx % 4
    xl, z, core = fs // 32, (fs // 2) % NZ, fs % 2
    step_z = 1 - 2 * core
    sends = []

    def dev_y(d):
        return (xh * 4 + (y + d) % 4, fs)

    def dev_ctx(flip, d):
        return (((xh + flip) % 2) * 4 + (y + d) % 4, fs)

    def dev_x(fh, fl):
        return (((xh + fh) % 2) * 4 + y, ((xl + fl) % 2) * 32 + fs % 32)

    x_opp = dev_ctx(1, 0)
    z_next = (ctx, xl * 32 + ((z + step_z + NZ) % NZ) * 2 + core)
    z_prev = (ctx, xl * 32 + ((z - step_z + NZ) % NZ) * 2 + core)
    sibling = (ctx, fs + step_z)

    def remote(src, dst, ss, rs, dev):
        return pltpu.make_async_remote_copy(
            src_ref=src, dst_ref=dst, send_sem=ss, recv_sem=rs, device_id=dev, device_id_type=MESH
        )

    def send(src, dst, ss, rs, dev):
        c = remote(src, dst, ss, rs, dev)
        c.start()
        sends.append(c)

    partners = [dev_ctx(f, d) for f in range(2) for d in range(4) if f or d]
    partners += [dev_x(0, 1), dev_x(1, 1), z_next, z_prev, sibling]
    barrier = pltpu.get_barrier_semaphore()
    for dev in partners:
        pl.semaphore_signal(barrier, inc=1, device_id=dev, device_id_type=MESH)

    wrow = pl.multiple_of(core * 32, 32)
    kcol = pl.multiple_of(y * 256, 256)
    qcol = pl.multiple_of(y * 512, 512)
    own = [
        pltpu.make_async_copy(w, wg.at[xh, xl, z, pl.ds(wrow, 32)], loc.at[0]),
        pltpu.make_async_copy(k.at[0, :, pl.ds(kcol, 256)], kbuf.at[ctx], loc.at[1]),
        pltpu.make_async_copy(v.at[0, :, pl.ds(kcol, 256)], vbuf.at[ctx], loc.at[2]),
        pltpu.make_async_copy(q.at[0, :, pl.ds(qcol, 512)], qbuf.at[y], loc.at[3]),
        pltpu.make_async_copy(pos, pbuf.at[ctx], loc.at[4]),
        pltpu.make_async_copy(hid.at[0], hbuf, loc.at[5]),
    ]
    for c in own:
        c.start()
    pl.semaphore_wait(barrier, len(partners))

    for i, (fh, fl) in enumerate(((0, 1), (1, 0), (1, 1))):
        send(w, wg.at[xh, xl, z, pl.ds(wrow, 32)], wx_s.at[i], wx_r.at[i], dev_x(fh, fl))
    for f in range(2):
        for d in range(4):
            if f or d:
                i = f * 4 + d
                send(pos, pbuf.at[ctx], p_s.at[i], p_r.at[i], dev_ctx(f, d))
    for d in (1, 3, 2):
        col = pl.multiple_of(((y + d) % 4) * 256, 256)
        send(k.at[0, :, pl.ds(col, 256)], kbuf.at[ctx], k_s.at[d], k_r.at[d], dev_y(d))
        send(v.at[0, :, pl.ds(col, 256)], vbuf.at[ctx], v_s.at[d], v_r.at[d], dev_y(d))
    send(k.at[0, :, pl.ds(kcol, 256)], kbuf.at[ctx], k_s.at[4], k_r.at[4], x_opp)
    send(v.at[0, :, pl.ds(kcol, 256)], vbuf.at[ctx], v_s.at[4], v_r.at[4], x_opp)
    for d in (1, 3, 2):
        col = pl.multiple_of(((y + d) % 4) * 512, 512)
        send(q.at[0, :, pl.ds(col, 512)], qbuf.at[y], q_s.at[d], q_r.at[d], dev_y(d))

    def arrived(dst, sem):
        remote(dst, dst, loc.at[6], sem, sibling).wait_recv()

    for i, (fh, fl) in enumerate(((0, 1), (1, 0), (1, 1))):
        arrived(wg.at[(xh + fh) % 2, (xl + fl) % 2, z, pl.ds(wrow, 32)], wx_r.at[i])
    own[0].wait()
    mine = wg.at[:, :, z, pl.ds(wrow, 32)]
    send(mine, mine, sb_s.at[8, 0], sb_r.at[8, 0], sibling)
    orow = pl.multiple_of((1 - core) * 32, 32)
    arrived(wg.at[:, :, z, pl.ds(orow, 32)], sb_r.at[8, 0])
    for h in range(2):
        send(wg.at[h, :, z], wg.at[h, :, z], rg_s.at[0, h], rg_r.at[0, h], z_next)

    for d in (1, 3, 2):
        src = xh * 4 + (y - d + 4) % 4
        arrived(kbuf.at[src], k_r.at[d])
        send(kbuf.at[src], kbuf.at[src], k_s.at[4 + d], k_r.at[4 + d], x_opp)
        arrived(vbuf.at[src], v_r.at[d])
        send(vbuf.at[src], vbuf.at[src], v_s.at[4 + d], v_r.at[4 + d], x_opp)

    def ring_step(s):
        zb = (z - step_z * (s + 1) + 2 * NZ) % NZ
        for h in range(2):

            def take(h=h):
                blk = wg.at[h, :, zb]
                arrived(blk, rg_r.at[s, h])
                if s < 6:
                    send(blk, blk, rg_s.at[s + 1, h], rg_r.at[s + 1, h], z_next)
                if s == 6:

                    @pl.when(core == h)
                    def _():
                        remote(blk, blk, rg_s.at[7, 0], rg_r.at[7, 0], z_next).start()

                send(blk, blk, sb_s.at[s, h], sb_r.at[s, h], sibling)

            take()

    def ring_last():
        zb = (z + NZ // 2) % NZ
        blk = wg.at[core, :, zb]
        arrived(blk, rg_r.at[7, 0])
        send(blk, blk, sb_s.at[7, 0], sb_r.at[7, 0], sibling)

    ring_step(0)
    ring_step(1)

    for c in own[1:]:
        c.wait()
    for f in range(2):
        for d in range(4):
            if f or d:
                arrived(pbuf.at[((xh + f) % 2) * 4 + (y - d + 4) % 4], p_r.at[f * 4 + d])
    for d in range(4):
        src = (1 - xh) * 4 + (y - d + 4) % 4
        arrived(kbuf.at[src], k_r.at[4 + d])
        arrived(vbuf.at[src], v_r.at[4 + d])

    def attend(t):
        prow = pbuf[xh * 4 + t].astype(jnp.float32)
        pcol = jnp.transpose(jnp.broadcast_to(prow, (TB, TB)), (1, 0))
        for c in range(8):
            key_pos = pbuf[c].astype(jnp.float32)
            bias[:, c * TB : (c + 1) * TB] = jnp.where(key_pos <= pcol, 0.0, -1e30)

        def head(h, _):
            g = h // 2
            col = pl.multiple_of(h * 128, 128)
            gcol = pl.multiple_of(g * 128, 128)
            keys = kbuf[:, :, pl.ds(gcol, 128)].reshape(8 * TB, 128)
            vals = vbuf[:, :, pl.ds(gcol, 128)].reshape(8 * TB, 128)
            qh = qbuf[t, :, pl.ds(col, 128)]
            s = lax.dot_general(qh, keys, (((1,), (1,)), ((), ())), preferred_element_type=jnp.float32)
            p = jnp.exp2(jnp.tanh(s * INNER) * OUTER + bias[...])
            den = jnp.sum(p, axis=-1, keepdims=True)
            num = jnp.dot(p.astype(jnp.bfloat16), vals, preferred_element_type=jnp.float32)
            att[y, pl.ds(pl.multiple_of(t * TB, TB), TB), pl.ds(col, 128)] = (num / den).astype(jnp.bfloat16)
            return 0

        lax.fori_loop(0, 4, head, 0)

    def att_rows(src, lo, n):
        return att.at[src, pl.ds(pl.multiple_of(lo, 64), n)]

    def att_forward(i):
        for side, d in enumerate((1, 3)):
            src = (y - d + 4) % 4
            t = (src + i) % 4
            arrived(att_rows(src, t * TB, TB), a_r.at[side, i])
            half = att_rows(src, t * TB + side * 64, 64)
            send(half, half, f_s.at[side, i], f_r.at[side, i], dev_y(d))

    for i in range(4):
        t = (y + i) % 4
        if i > 0:
            dq = 4 - i
            arrived(qbuf.at[t], q_r.at[dq])
        attend(t)
        blk = att_rows(y, t * TB, TB)
        for side, d in enumerate((1, 3)):
            send(blk, blk, a_s.at[side, i], a_r.at[side, i], dev_y(d))
        if i > 0:
            att_forward(i - 1)
        ring_step(2 + i)
    att_forward(3)
    ring_step(6)
    ring_last()
    for s in range(7):
        zb = (z + step_z * (s + 1) + 2 * NZ) % NZ
        for h in range(2):
            arrived(wg.at[h, :, zb], sb_r.at[s, h])
    arrived(wg.at[1 - core, :, (z + NZ // 2) % NZ], sb_r.at[7, 0])

    def project(src, first):
        wl, wz = src // 2, (src % 2) * 8

        def part(i, _):
            b, m = i // 2, pl.multiple_of((i % 2) * 256, 256)
            wb = wg[b, wl, pl.ds(wz, 8)].reshape(512, CB)
            r = jnp.dot(att[src, pl.ds(m, 256)], wb, preferred_element_type=jnp.float32)
            if first:
                acc[b, pl.ds(m, 256)] = r
            else:
                acc[b, pl.ds(m, 256)] += r
            return 0

        lax.fori_loop(0, 4, part, 0)

    project(y, True)
    project((y + 3) % 4, False)
    project((y + 1) % 4, False)
    far = (y + 2) % 4
    for i in range(4):
        for side, d in enumerate((1, 3)):
            t = (far + i) % 4
            arrived(att_rows(far, t * TB + side * 64, 64), f_r.at[side, i])
    wl, wz = far // 2, (far % 2) * 8
    for b in range(2):

        def last(m, _, b=b):
            m = pl.multiple_of(m * 256, 256)
            wb = wg[b, wl, pl.ds(wz, 8)].reshape(512, CB)
            r = jnp.dot(att[far, pl.ds(m, 256)], wb, preferred_element_type=jnp.float32)
            obuf[b, pl.ds(m, 256)] = (acc[b, pl.ds(m, 256)] + r).astype(jnp.bfloat16)
            return 0

        lax.fori_loop(0, 2, last, 0)
        for d in (2, 1, 3):
            t = (y + d) % 4
            src = obuf.at[b, pl.ds(pl.multiple_of(t * TB, TB), TB)]
            send(src, rows.at[b * 4 + y], o_s.at[b, d], o_r.at[b, d], dev_y(d))
        rows[b * 4 + y] = obuf[b, pl.ds(pl.multiple_of(y * TB, TB), TB)]
    for b in range(2):
        for d in (1, 3, 2):
            arrived(rows.at[b * 4 + (y - d + 4) % 4], o_r.at[b, d])

    def norm(i, _):
        r = pl.ds(pl.multiple_of(i * 32, 32), 32)
        ss = jnp.zeros((32, 1), jnp.float32)
        for c in range(8):
            x = rows[c, r].astype(jnp.float32)
            ss += jnp.sum(x * x, axis=-1, keepdims=True)
        scale = lax.rsqrt(ss * (1.0 / D) + NORM_EPS)
        for c in range(8):
            cols = slice(c * CB, (c + 1) * CB)
            x = rows[c, r].astype(jnp.float32) * scale * gain[:, cols]
            out[0, r, cols] = (hbuf[r, cols].astype(jnp.float32) + x).astype(jnp.bfloat16)
        return 0

    lax.fori_loop(0, 4, norm, 0)

    for c in sends:
        c.wait_send()
    last_blk = wg.at[core, :, (z - step_z * 7 + 2 * NZ) % NZ]
    remote(last_blk, last_blk, rg_s.at[7, 0], rg_r.at[7, 0], z_next).wait_send()


def shards(hidden_rows, query_proj, key_proj, value_proj, order_pos, post_gain, out_weight):
    hbm = pl.BlockSpec(memory_space=pl.ANY)
    vmem = pl.BlockSpec(memory_space=pltpu.VMEM)
    bf16, f32, dma = jnp.bfloat16, jnp.float32, pltpu.SemaphoreType.DMA
    return pl.pallas_call(
        body,
        name="sublayer",
        out_shape=jax.ShapeDtypeStruct((1, TB, D), bf16),
        in_specs=[hbm, hbm, hbm, hbm, hbm, vmem, hbm],
        out_specs=vmem,
        scratch_shapes=[
            pltpu.VMEM((4, TB, 512), bf16),
            pltpu.VMEM((8, TB, 256), bf16),
            pltpu.VMEM((8, TB, 256), bf16),
            pltpu.VMEM((8, 1, TB), jnp.int32),
            pltpu.VMEM((TB, 8 * TB), f32),
            pltpu.VMEM((4, 512, 512), bf16),
            pltpu.VMEM((2, 2, NZ, 64, CB), bf16),
            pltpu.VMEM((2, 512, CB), f32),
            pltpu.VMEM((2, 512, CB), bf16),
            pltpu.VMEM((8, TB, CB), bf16),
            pltpu.VMEM((TB, D), bf16),
            dma((7,)),
            dma((4,)), dma((4,)),
            dma((8,)), dma((8,)),
            dma((8,)), dma((8,)),
            dma((8,)), dma((8,)),
            dma((3,)), dma((3,)),
            dma((8, 2)), dma((8, 2)),
            dma((9, 2)), dma((9, 2)),
            dma((2, 4)), dma((2, 4)),
            dma((2, 4)), dma((2, 4)),
            dma((2, 4)), dma((2, 4)),
        ],
        compiler_params=pltpu.CompilerParams(
            collective_id=0, has_side_effects=True, vmem_limit_bytes=48 << 20
        ),
    )(hidden_rows, query_proj, key_proj, value_proj, order_pos, post_gain.reshape(1, D), out_weight)


def solution(mesh):
    placed = (
        P("fsdp", "ctx", None),
        P("fsdp", "ctx", None),
        P("fsdp", "ctx", None),
        P("fsdp", "ctx", None),
        P("fsdp", "ctx"),
        P(),
        P("fsdp", "ctx"),
    )
    return jax.shard_map(
        shards, mesh=mesh, in_specs=placed, out_specs=P("fsdp", "ctx", None), check_vma=False
    )
```

```python
import jax
import jax.numpy as jnp
from jax import lax
from jax.experimental import pallas as pl
from jax.experimental.pallas import tpu as pltpu
from jax.sharding import PartitionSpec as P

D = 4608
OTHERS = [(0, 1), (1, 0), (1, 1)]
TB = 128
HB = 64
CB = 576
CP = 2 * CB
NZ = 16
INNER = 1.0 / 600.0
OUTER = 50.0 * 1.4426950408889634
NORM_EPS = 1e-06
MESH = pl.DeviceIdType.MESH
AWAY = [0, 1, -1, 2, -2, 3, -3, 4, -4, 5, -5, 6, -6, 7, -7, 8]


def body(
    hid, q, k, v, pos, gain, w, out,
    qbuf, kbuf, vbuf, pbuf, bias, att, wst, wf, wg, obuf, rows, hbuf, gbuf, res,
    loc, q_s, q_r, k_s, k_r, v_s, v_r, p_s, p_r, wz_s, wz_r, wx_s, wx_r,
    sb_s, sb_r, a_s, a_r, f_s, f_r, o_s, o_r,
):
    ctx = lax.axis_index("ctx")
    fs = lax.axis_index("fsdp")
    xh, y = ctx // 4, ctx % 4
    xl, z, core = fs // 32, (fs // 2) % NZ, fs % 2
    sends = []

    def dev_y(d):
        return (xh * 4 + (y + d) % 4, fs)

    def dev_ctx(flip, d):
        return (((xh + flip) % 2) * 4 + (y + d) % 4, fs)

    def dev_x(fh, fl):
        return (((xh + fh) % 2) * 4 + y, ((xl + fl) % 2) * 32 + fs % 32)

    x_opp = dev_ctx(1, 0)
    sibling = (ctx, fs + 1 - 2 * core)

    def dev_z(d):
        return (ctx, xl * 32 + ((z + d + NZ) % NZ) * 2 + core)

    def remote(src, dst, ss, rs, dev):
        return pltpu.make_async_remote_copy(
            src_ref=src, dst_ref=dst, send_sem=ss, recv_sem=rs, device_id=dev, device_id_type=MESH
        )

    def send(src, dst, ss, rs, dev):
        c = remote(src, dst, ss, rs, dev)
        c.start()
        sends.append(c)

    def arrived(dst, sem):
        remote(dst, dst, loc.at[6], sem, sibling).wait_recv()

    partners = [dev_ctx(f, d) for f in range(2) for d in range(4) if f or d]
    partners += [dev_x(0, 1), dev_x(1, 1), sibling] + [dev_z(d) for d in AWAY[1:]]
    barrier = pltpu.get_barrier_semaphore()
    for dev in partners:
        pl.semaphore_signal(barrier, inc=1, device_id=dev, device_id_type=MESH)

    kcol = pl.multiple_of(y * 256, 256)
    qcol = pl.multiple_of(y * 512, 512)
    own = [
        pltpu.make_async_copy(w, wst, loc.at[0]),
        pltpu.make_async_copy(k.at[0, :, pl.ds(kcol, 256)], kbuf.at[ctx], loc.at[1]),
        pltpu.make_async_copy(v.at[0, :, pl.ds(kcol, 256)], vbuf.at[ctx], loc.at[2]),
        pltpu.make_async_copy(q.at[0, :, pl.ds(qcol, 512)], qbuf.at[y], loc.at[3]),
        pltpu.make_async_copy(pos, pbuf.at[ctx], loc.at[4]),
        pltpu.make_async_copy(hid.at[0], hbuf, loc.at[5]),
        pltpu.make_async_copy(gain, gbuf.at[0], loc.at[7]),
    ]
    for c in own:
        c.start()
    own[0].wait()
    wf[xh, xl, core, 0] = jnp.concatenate([wst[0:16], wst[16:32]], axis=1)
    pl.semaphore_wait(barrier, len(partners))

    for d in (1, 3, 2):
        col = pl.multiple_of(((y + d) % 4) * 256, 256)
        send(k.at[0, :, pl.ds(col, 256)], kbuf.at[ctx], k_s.at[d], k_r.at[d], dev_y(d))
        send(v.at[0, :, pl.ds(col, 256)], vbuf.at[ctx], v_s.at[d], v_r.at[d], dev_y(d))
    send(k.at[0, :, pl.ds(kcol, 256)], kbuf.at[ctx], k_s.at[4], k_r.at[4], x_opp)
    send(v.at[0, :, pl.ds(kcol, 256)], vbuf.at[ctx], v_s.at[4], v_r.at[4], x_opp)
    for f in range(2):
        for d in range(4):
            if f or d:
                i = f * 4 + d
                send(pos, pbuf.at[ctx], p_s.at[i], p_r.at[i], dev_ctx(f, d))

    own_w = wf.at[xh, xl, core, 0]
    for r, d in enumerate(AWAY):
        if r:
            back = AWAY.index(-d if d < 8 else 8)
            send(own_w, wf.at[xh, xl, core, back], wz_s.at[r], wz_r.at[back], dev_z(d))
    for d in (1, 3, 2):
        col = pl.multiple_of(((y + d) % 4) * 512, 512)
        send(q.at[0, :, pl.ds(col, 512)], qbuf.at[y], q_s.at[d], q_r.at[d], dev_y(d))

    def forward_kv(d):
        src = xh * 4 + (y - d + 4) % 4
        arrived(kbuf.at[src], k_r.at[d])
        send(kbuf.at[src], kbuf.at[src], k_s.at[4 + d], k_r.at[4 + d], x_opp)
        arrived(vbuf.at[src], v_r.at[d])
        send(vbuf.at[src], vbuf.at[src], v_s.at[4 + d], v_r.at[4 + d], x_opp)

    forward_kv(1)
    forward_kv(3)
    forward_kv(2)

    def batch(ref_h, ref_l, c, b):
        return wf.at[ref_h, ref_l, c, pl.ds(4 * b, 4)]

    def weights_z(b):
        for r in range(max(4 * b, 1), 4 * b + 4):
            arrived(wf.at[xh, xl, core, r], wz_r.at[r])
        src = batch(xh, xl, core, b)
        for i, (fh, fl) in enumerate(OTHERS):
            send(src, src, wx_s.at[i, b], wx_r.at[i, b], dev_x(fh, fl))
        send(src, src, sb_s.at[3, b], sb_r.at[3, b], sibling)

    def weights_x(b):
        for i, (fh, fl) in enumerate(OTHERS):
            src = batch((xh + fh) % 2, (xl + fl) % 2, core, b)
            arrived(src, wx_r.at[i, b])
            send(src, src, sb_s.at[i, b], sb_r.at[i, b], sibling)

    def unfold(b):
        for i, (fh, fl) in enumerate(OTHERS + [(0, 0)]):
            arrived(batch((xh + fh) % 2, (xl + fl) % 2, 1 - core, b), sb_r.at[i, b])

        def piece(i, _):
            l, c = i // 2, i % 2
            for r in range(4 * b, 4 * b + 4):
                zb = (z + AWAY[r] + NZ) % NZ
                lo, hi = wf[0, l, c, r], wf[1, l, c, r]
                top = pl.multiple_of(c * 32, 32)
                wg[l, zb, pl.ds(top, 16)] = jnp.concatenate([lo[:, :CB], hi[:, :CB]], axis=1)
                wg[l, zb, pl.ds(top + 16, 16)] = jnp.concatenate([lo[:, CB:], hi[:, CB:]], axis=1)
            return 0

        lax.fori_loop(0, 4, piece, 0)

    for f in range(2):
        for d in range(4):
            if f or d:
                arrived(pbuf.at[((xh + f) % 2) * 4 + (y - d + 4) % 4], p_r.at[f * 4 + d])
    own[4].wait()
    for t in range(4):
        prow = pbuf[xh * 4 + t].astype(jnp.float32)
        pcol = jnp.transpose(jnp.broadcast_to(prow, (TB, TB)), (1, 0))
        for c in range(8):
            seen = jnp.where(pbuf[c].astype(jnp.float32) <= pcol, 0.0, -1e30)
            for p in range(2):
                bias[p, t * HB : (t + 1) * HB, c * TB : (c + 1) * TB] = seen[p * HB : (p + 1) * HB]

    weights_z(0)
    for c in own[1:4] + own[5:]:
        c.wait()
    for d in (1, 3, 2):
        arrived(qbuf.at[(y - d + 4) % 4], q_r.at[d])
    weights_z(1)
    for d in range(4):
        src = (1 - xh) * 4 + (y - d + 4) % 4
        arrived(kbuf.at[src], k_r.at[4 + d])
        arrived(vbuf.at[src], v_r.at[4 + d])

    def attend(p, h):
        gcol = pl.multiple_of((h // 2) * 128, 128)
        qh = qbuf[:, pl.ds(pl.multiple_of(p * HB, HB), HB), pl.ds(pl.multiple_of(h * 128, 128), 128)]
        qh = qh.reshape(4 * HB, 128)
        num = den = 0.0
        for c in range(4):
            keys = kbuf[2 * c : 2 * c + 2, :, pl.ds(gcol, 128)].reshape(2 * TB, 128)
            vals = vbuf[2 * c : 2 * c + 2, :, pl.ds(gcol, 128)].reshape(2 * TB, 128)
            s = lax.dot_general(qh, keys, (((1,), (1,)), ((), ())), preferred_element_type=jnp.float32)
            e = jnp.exp2(jnp.tanh(s * INNER) * OUTER + bias[p, :, c * 256 : (c + 1) * 256])
            den += e[:, :128] + e[:, 128:]
            num += jnp.dot(e.astype(jnp.bfloat16), vals, preferred_element_type=jnp.float32)
        den = jnp.sum(den, axis=-1, keepdims=True)
        att[y, p, h] = (num / den).astype(jnp.bfloat16)

    def att_forward(u):
        p, h = u // 4, u % 4
        for side, d in enumerate((1, 3)):
            src = (y - d + 4) % 4
            arrived(att.at[src, p, h], a_r.at[side, u])
            half = att.at[src, p, h, pl.ds(side * TB, TB)]
            remote(half, half, f_s.at[side, u], f_r.at[side, u], dev_y(d)).start()

    def unit(u, _):
        p, h = u // 4, u % 4
        attend(p, h)
        blk = att.at[y, p, h]
        for side, d in enumerate((1, 3)):
            remote(blk, blk, a_s.at[side, u], a_r.at[side, u], dev_y(d)).start()

        @pl.when(u >= 4)
        def _():
            att_forward(u - 4)

        return 0

    lax.fori_loop(0, 4, unit, 0)
    weights_z(2)
    weights_x(0)
    lax.fori_loop(4, 8, unit, 0)
    weights_z(3)
    weights_x(1)
    unfold(0)
    att_forward(4)
    att_forward(5)

    far = (y + 2) % 4

    def far_arrived(p):
        for h in range(4):
            for side in range(2):
                arrived(att.at[far, p, h, pl.ds(side * TB, TB)], f_r.at[side, p * 4 + h])

    def project(p):
        def cols(n, _):
            n = pl.multiple_of(n * 384, 384)
            r = 0.0
            for src in range(4):
                a = jnp.concatenate([att[src, p, h] for h in range(4)], axis=1)
                wb = wg[src // 2, (src % 2) * 8 : (src % 2) * 8 + 8, :, pl.ds(n, 384)].reshape(512, 384)
                r += jnp.dot(a, wb, preferred_element_type=jnp.float32)
            obuf[p, :, :, pl.ds(n, 384)] = r.astype(jnp.bfloat16).reshape(4, HB, 384)
            return 0

        lax.fori_loop(0, 3, cols, 0)
        for d in (2, 1, 3):
            dst = rows.at[p, y]
            send(obuf.at[p, (y + d) % 4], dst, o_s.at[p, d], o_r.at[p, d], dev_y(d))
        rows[p, y] = obuf[p, y]

    def norm(p):
        for d in (1, 3, 2):
            arrived(rows.at[p, (y - d + 4) % 4], o_r.at[p, d])

        def piece(i, _):
            r = pl.ds(pl.multiple_of(i * 32, 32), 32)
            t = pl.ds(pl.multiple_of(p * HB + i * 32, 32), 32)
            ss = jnp.zeros((32, 1), jnp.float32)
            for c in range(4):
                x = rows[p, c, r].astype(jnp.float32)
                ss += jnp.sum(x * x, axis=-1, keepdims=True)
            scale = lax.rsqrt(ss * (1.0 / D) + NORM_EPS)
            for c in range(4):
                x = rows[p, c, r].astype(jnp.float32) * scale
                for b in range(2):
                    cols = slice(b * 4 * CB + c * CB, b * 4 * CB + (c + 1) * CB)
                    n = x[:, b * CB : (b + 1) * CB] * gbuf[:, cols]
                    res[t, cols] = (hbuf[t, cols].astype(jnp.float32) + n).astype(jnp.bfloat16)
            return 0

        lax.fori_loop(0, 2, piece, 0)
        done = pl.ds(p * HB, HB)
        return pltpu.make_async_copy(res.at[done], out.at[0, done], loc.at[8 + p])

    weights_x(2)
    unfold(1)
    att_forward(6)
    weights_x(3)
    unfold(2)
    att_forward(7)
    far_arrived(0)
    unfold(3)
    project(0)
    far_arrived(1)
    project(1)
    first = norm(0)
    first.start()
    second = norm(1)
    second.start()
    first.wait()
    second.wait()

    for c in sends:
        c.wait_send()
    for u in range(8):
        for side in range(2):
            blk = att.at[0, 0, 0]
            remote(blk, blk, a_s.at[side, u], loc.at[6], sibling).wait_send()
            blk = att.at[0, 0, 0, pl.ds(0, TB)]
            remote(blk, blk, f_s.at[side, u], loc.at[6], sibling).wait_send()


def shards(hidden_rows, query_proj, key_proj, value_proj, order_pos, post_gain, out_weight):
    hbm = pl.BlockSpec(memory_space=pl.ANY)
    bf16, f32, dma = jnp.bfloat16, jnp.float32, pltpu.SemaphoreType.DMA
    return pl.pallas_call(
        body,
        name="sublayer",
        out_shape=jax.ShapeDtypeStruct((1, TB, D), bf16),
        in_specs=[hbm] * 7,
        out_specs=hbm,
        scratch_shapes=[
            pltpu.VMEM((4, TB, 512), bf16),
            pltpu.VMEM((8, TB, 256), bf16),
            pltpu.VMEM((8, TB, 256), bf16),
            pltpu.VMEM((8, 1, TB), jnp.int32),
            pltpu.VMEM((2, 4 * HB, 8 * TB), f32),
            pltpu.VMEM((4, 2, 4, 4 * HB, 128), bf16),
            pltpu.VMEM((32, CB), bf16),
            pltpu.VMEM((2, 2, 2, NZ, 16, CP), bf16),
            pltpu.VMEM((2, NZ, 64, CP), bf16),
            pltpu.VMEM((2, 4, HB, CP), bf16),
            pltpu.VMEM((2, 4, HB, CP), bf16),
            pltpu.VMEM((TB, D), bf16),
            pltpu.VMEM((1, D), f32),
            pltpu.VMEM((TB, D), bf16),
            dma((10,)),
            dma((4,)), dma((4,)),
            dma((8,)), dma((8,)),
            dma((8,)), dma((8,)),
            dma((8,)), dma((8,)),
            dma((NZ,)), dma((NZ,)),
            dma((3, 4)), dma((3, 4)),
            dma((4, 4)), dma((4, 4)),
            dma((2, 8)), dma((2, 8)),
            dma((2, 8)), dma((2, 8)),
            dma((2, 4)), dma((2, 4)),
        ],
        compiler_params=pltpu.CompilerParams(
            collective_id=0, has_side_effects=True, vmem_limit_bytes=60 << 20
        ),
    )(hidden_rows, query_proj, key_proj, value_proj, order_pos, post_gain, out_weight)


def solution(mesh):
    placed = (
        P("fsdp", "ctx", None),
        P("fsdp", "ctx", None),
        P("fsdp", "ctx", None),
        P("fsdp", "ctx", None),
        P("fsdp", "ctx"),
        P(),
        P("fsdp", "ctx"),
    )
    return jax.shard_map(
        shards, mesh=mesh, in_specs=placed, out_specs=P("fsdp", "ctx", None), check_vma=False
    )
```

```python
import jax
import jax.numpy as jnp
from jax import lax
from jax.experimental import pallas as pl
from jax.experimental.pallas import tpu as pltpu
from jax.sharding import PartitionSpec as P

D = 4608
TB = 128
HB = 64
CB = 576
CP = 2 * CB
NZ = 16
INNER = 1.0 / 600.0
OUTER = 50.0 * 1.4426950408889634
NORM_EPS = 1e-06
MESH = pl.DeviceIdType.MESH
AWAY = [0, 1, -1, 2, -2, 3, -3, 4, -4, 5, -5, 6, -6, 7, -7, 8]


def body(
    hid, q, k, v, pos, gain, w, out,
    qbuf, kbuf, vbuf, pbuf, bias, att, wst, wf, wg, obuf, rows, hbuf, gbuf, res,
    loc, q_s, q_r, k_s, k_r, v_s, v_r, p_s, p_r, wz_s, wz_r, wx_s, wx_r,
    sb_s, sb_r, a_s, a_r, f_s, f_r, o_s, o_r,
):
    ctx = lax.axis_index("ctx")
    fs = lax.axis_index("fsdp")
    xh, y = ctx // 4, ctx % 4
    xl, z, core = fs // 32, (fs // 2) % NZ, fs % 2
    sends = []

    def dev_y(d):
        return (xh * 4 + (y + d) % 4, fs)

    def dev_ctx(flip, d):
        return (((xh + flip) % 2) * 4 + (y + d) % 4, fs)

    def at_x(d):
        return (xh * 2 + xl + d + 4) % 4

    def dev_x(d):
        return ((at_x(d) // 2) * 4 + y, (at_x(d) % 2) * 32 + fs % 32)

    x_opp = dev_ctx(1, 0)
    sibling = (ctx, fs + 1 - 2 * core)

    def dev_z(d):
        return (ctx, xl * 32 + ((z + d + NZ) % NZ) * 2 + core)

    def remote(src, dst, ss, rs, dev):
        return pltpu.make_async_remote_copy(
            src_ref=src, dst_ref=dst, send_sem=ss, recv_sem=rs, device_id=dev, device_id_type=MESH
        )

    def send(src, dst, ss, rs, dev):
        c = remote(src, dst, ss, rs, dev)
        c.start()
        sends.append(c)

    def arrived(dst, sem):
        remote(dst, dst, loc.at[6], sem, sibling).wait_recv()

    partners = [dev_ctx(f, d) for f in range(2) for d in range(4) if f or d]
    partners += [dev_x(1), dev_x(-1), sibling] + [dev_z(d) for d in AWAY[1:]]
    barrier = pltpu.get_barrier_semaphore()
    for dev in partners:
        pl.semaphore_signal(barrier, inc=1, device_id=dev, device_id_type=MESH)

    kcol = pl.multiple_of(y * 256, 256)
    qcol = pl.multiple_of(y * 512, 512)
    own = [
        pltpu.make_async_copy(w, wst, loc.at[0]),
        pltpu.make_async_copy(k.at[0, :, pl.ds(kcol, 256)], kbuf.at[ctx], loc.at[1]),
        pltpu.make_async_copy(v.at[0, :, pl.ds(kcol, 256)], vbuf.at[ctx], loc.at[2]),
        pltpu.make_async_copy(q.at[0, :, pl.ds(qcol, 512)], qbuf.at[y], loc.at[3]),
        pltpu.make_async_copy(pos, pbuf.at[ctx], loc.at[4]),
        pltpu.make_async_copy(hid.at[0], hbuf, loc.at[5]),
        pltpu.make_async_copy(gain, gbuf.at[0], loc.at[7]),
    ]
    for c in own:
        c.start()
    own[0].wait()
    wf[xh, xl, core, 0] = jnp.concatenate([wst[0:16], wst[16:32]], axis=1)
    pl.semaphore_wait(barrier, len(partners))

    for d in (1, 3, 2):
        col = pl.multiple_of(((y + d) % 4) * 256, 256)
        send(k.at[0, :, pl.ds(col, 256)], kbuf.at[ctx], k_s.at[d], k_r.at[d], dev_y(d))
        send(v.at[0, :, pl.ds(col, 256)], vbuf.at[ctx], v_s.at[d], v_r.at[d], dev_y(d))
    send(k.at[0, :, pl.ds(kcol, 256)], kbuf.at[ctx], k_s.at[4], k_r.at[4], x_opp)
    send(v.at[0, :, pl.ds(kcol, 256)], vbuf.at[ctx], v_s.at[4], v_r.at[4], x_opp)
    for f in range(2):
        for d in range(4):
            if f or d:
                i = f * 4 + d
                send(pos, pbuf.at[ctx], p_s.at[i], p_r.at[i], dev_ctx(f, d))

    def away(d):
        return AWAY.index(d if d < 8 else 8) if d > -8 else AWAY.index(8)

    own_w = wf.at[xh, xl, core, 0]
    for d in (1, -1, 4, -4, 2, -2, 3, -3):
        send(own_w, wf.at[xh, xl, core, away(-d)], wz_s.at[away(d)], wz_r.at[away(-d)], dev_z(d))
    for d in (1, 3, 2):
        col = pl.multiple_of(((y + d) % 4) * 512, 512)
        send(q.at[0, :, pl.ds(col, 512)], qbuf.at[y], q_s.at[d], q_r.at[d], dev_y(d))

    def forward_kv(d):
        src = xh * 4 + (y - d + 4) % 4
        arrived(kbuf.at[src], k_r.at[d])
        send(kbuf.at[src], kbuf.at[src], k_s.at[4 + d], k_r.at[4 + d], x_opp)
        arrived(vbuf.at[src], v_r.at[d])
        send(vbuf.at[src], vbuf.at[src], v_s.at[4 + d], v_r.at[4 + d], x_opp)

    forward_kv(1)
    forward_kv(3)
    for side in (1, -1):
        blk = wf.at[xh, xl, core, away(-4 * side)]
        arrived(blk, wz_r.at[away(-4 * side)])
        for e in (4, 3, 2, 1) if side > 0 else (3, 2, 1):
            r = away(-(4 + e) * side)
            send(blk, wf.at[xh, xl, core, r], wz_s.at[away((4 + e) * side)], wz_r.at[r], dev_z(e * side))
    forward_kv(2)

    def blocks(d, c, first, n):
        return wf.at[at_x(d) // 2, at_x(d) % 2, c, pl.ds(first, n)]

    def weights_z(b):
        for r in range(max(4 * b, 1), 4 * b + 4):
            if AWAY[r] not in (4, -4):
                arrived(wf.at[xh, xl, core, r], wz_r.at[r])
        src = blocks(0, core, 4 * b, 4)
        for side, d in enumerate((1, -1)):
            send(src, src, wx_s.at[side, b], wx_r.at[side, b], dev_x(d))
        send(src, src, sb_s.at[0, b], sb_r.at[0, b], sibling)

    def weights_x(b):
        for side, d in enumerate((1, -1)):
            src = blocks(-d, core, 4 * b, 4)
            arrived(src, wx_r.at[side, b])
            half = blocks(-d, core, 4 * b + 2 * side, 2)
            send(half, half, wx_s.at[2 + side, b], wx_r.at[2 + side, b], dev_x(d))
            send(src, src, sb_s.at[1 + side, b], sb_r.at[1 + side, b], sibling)

    def weights_far(b):
        for side in range(2):
            half = blocks(2, core, 4 * b + 2 * side, 2)
            arrived(half, wx_r.at[2 + side, b])
            send(half, half, sb_s.at[3 + side, b], sb_r.at[3 + side, b], sibling)

    def unfold(b):
        for i, d in enumerate((0, -1, 1)):
            arrived(blocks(d, 1 - core, 4 * b, 4), sb_r.at[i, b])
        for side in range(2):
            arrived(blocks(2, 1 - core, 4 * b + 2 * side, 2), sb_r.at[3 + side, b])

        def piece(i, _):
            l, c = i // 2, i % 2
            for r in range(4 * b, 4 * b + 4):
                zb = (z + AWAY[r] + NZ) % NZ
                lo, hi = wf[0, l, c, r], wf[1, l, c, r]
                top = pl.multiple_of(c * 32, 32)
                wg[l, zb, pl.ds(top, 16)] = jnp.concatenate([lo[:, :CB], hi[:, :CB]], axis=1)
                wg[l, zb, pl.ds(top + 16, 16)] = jnp.concatenate([lo[:, CB:], hi[:, CB:]], axis=1)
            return 0

        lax.fori_loop(0, 4, piece, 0)

    for f in range(2):
        for d in range(4):
            if f or d:
                arrived(pbuf.at[((xh + f) % 2) * 4 + (y - d + 4) % 4], p_r.at[f * 4 + d])
    own[4].wait()
    for t in range(4):
        prow = pbuf[xh * 4 + t].astype(jnp.float32)
        pcol = jnp.transpose(jnp.broadcast_to(prow, (TB, TB)), (1, 0))
        for c in range(8):
            seen = jnp.where(pbuf[c].astype(jnp.float32) <= pcol, 0.0, -1e30)
            for p in range(2):
                bias[p, t * HB : (t + 1) * HB, c * TB : (c + 1) * TB] = seen[p * HB : (p + 1) * HB]

    weights_z(0)
    for c in own[1:4] + own[5:]:
        c.wait()
    for d in (1, 3, 2):
        arrived(qbuf.at[(y - d + 4) % 4], q_r.at[d])
    weights_z(1)
    for d in range(4):
        src = (1 - xh) * 4 + (y - d + 4) % 4
        arrived(kbuf.at[src], k_r.at[4 + d])
        arrived(vbuf.at[src], v_r.at[4 + d])

    def attend(p, h):
        gcol = pl.multiple_of((h // 2) * 128, 128)
        qh = qbuf[:, pl.ds(pl.multiple_of(p * HB, HB), HB), pl.ds(pl.multiple_of(h * 128, 128), 128)]
        qh = qh.reshape(4 * HB, 128)
        num = den = 0.0
        for c in range(4):
            keys = kbuf[2 * c : 2 * c + 2, :, pl.ds(gcol, 128)].reshape(2 * TB, 128)
            vals = vbuf[2 * c : 2 * c + 2, :, pl.ds(gcol, 128)].reshape(2 * TB, 128)
            s = lax.dot_general(qh, keys, (((1,), (1,)), ((), ())), preferred_element_type=jnp.float32)
            e = jnp.exp2(jnp.tanh(s * INNER) * OUTER + bias[p, :, c * 256 : (c + 1) * 256])
            den += e[:, :128] + e[:, 128:]
            num += jnp.dot(e.astype(jnp.bfloat16), vals, preferred_element_type=jnp.float32)
        den = jnp.sum(den, axis=-1, keepdims=True)
        att[y, p, h] = (num / den).astype(jnp.bfloat16)

    def att_forward(u):
        p, h = u // 4, u % 4
        for side, d in enumerate((1, 3)):
            src = (y - d + 4) % 4
            arrived(att.at[src, p, h], a_r.at[side, u])
            half = att.at[src, p, h, pl.ds(side * TB, TB)]
            remote(half, half, f_s.at[side, u], f_r.at[side, u], dev_y(d)).start()

    def unit(u, _):
        p, h = u // 4, u % 4
        attend(p, h)
        blk = att.at[y, p, h]
        for side, d in enumerate((1, 3)):
            remote(blk, blk, a_s.at[side, u], a_r.at[side, u], dev_y(d)).start()

        @pl.when(u >= 4)
        def _():
            att_forward(u - 4)

        return 0

    lax.fori_loop(0, 2, unit, 0)
    weights_x(0)
    lax.fori_loop(2, 4, unit, 0)
    weights_z(2)
    lax.fori_loop(4, 6, unit, 0)
    weights_x(1)
    weights_z(3)
    lax.fori_loop(6, 8, unit, 0)
    weights_far(0)
    weights_x(2)
    att_forward(4)
    weights_far(1)
    unfold(0)
    att_forward(5)
    weights_x(3)

    far = (y + 2) % 4

    def far_arrived(p):
        for h in range(4):
            for side in range(2):
                arrived(att.at[far, p, h, pl.ds(side * TB, TB)], f_r.at[side, p * 4 + h])

    def project(p):
        def cols(n, _):
            n = pl.multiple_of(n * 384, 384)
            r = 0.0
            for src in range(4):
                a = jnp.concatenate([att[src, p, h] for h in range(4)], axis=1)
                wb = wg[src // 2, (src % 2) * 8 : (src % 2) * 8 + 8, :, pl.ds(n, 384)].reshape(512, 384)
                r += jnp.dot(a, wb, preferred_element_type=jnp.float32)
            obuf[p, :, :, pl.ds(n, 384)] = r.astype(jnp.bfloat16).reshape(4, HB, 384)
            return 0

        lax.fori_loop(0, 3, cols, 0)
        for d in (2, 1, 3):
            dst = rows.at[p, y]
            send(obuf.at[p, (y + d) % 4], dst, o_s.at[p, d], o_r.at[p, d], dev_y(d))
        rows[p, y] = obuf[p, y]

    def norm(p):
        for d in (1, 3, 2):
            arrived(rows.at[p, (y - d + 4) % 4], o_r.at[p, d])

        def piece(i, _):
            r = pl.ds(pl.multiple_of(i * 32, 32), 32)
            t = pl.ds(pl.multiple_of(p * HB + i * 32, 32), 32)
            ss = jnp.zeros((32, 1), jnp.float32)
            for c in range(4):
                x = rows[p, c, r].astype(jnp.float32)
                ss += jnp.sum(x * x, axis=-1, keepdims=True)
            scale = lax.rsqrt(ss * (1.0 / D) + NORM_EPS)
            for c in range(4):
                x = rows[p, c, r].astype(jnp.float32) * scale
                for b in range(2):
                    cols = slice(b * 4 * CB + c * CB, b * 4 * CB + (c + 1) * CB)
                    n = x[:, b * CB : (b + 1) * CB] * gbuf[:, cols]
                    res[t, cols] = (hbuf[t, cols].astype(jnp.float32) + n).astype(jnp.bfloat16)
            return 0

        lax.fori_loop(0, 2, piece, 0)
        done = pl.ds(p * HB, HB)
        return pltpu.make_async_copy(res.at[done], out.at[0, done], loc.at[8 + p])

    weights_far(2)
    unfold(1)
    att_forward(6)
    weights_far(3)
    unfold(2)
    att_forward(7)
    far_arrived(0)
    unfold(3)
    project(0)
    far_arrived(1)
    project(1)
    first = norm(0)
    first.start()
    second = norm(1)
    second.start()
    first.wait()
    second.wait()

    for c in sends:
        c.wait_send()
    for u in range(8):
        for side in range(2):
            blk = att.at[0, 0, 0]
            remote(blk, blk, a_s.at[side, u], loc.at[6], sibling).wait_send()
            blk = att.at[0, 0, 0, pl.ds(0, TB)]
            remote(blk, blk, f_s.at[side, u], loc.at[6], sibling).wait_send()


def shards(hidden_rows, query_proj, key_proj, value_proj, order_pos, post_gain, out_weight):
    hbm = pl.BlockSpec(memory_space=pl.ANY)
    bf16, f32, dma = jnp.bfloat16, jnp.float32, pltpu.SemaphoreType.DMA
    return pl.pallas_call(
        body,
        name="sublayer",
        out_shape=jax.ShapeDtypeStruct((1, TB, D), bf16),
        in_specs=[hbm] * 7,
        out_specs=hbm,
        scratch_shapes=[
            pltpu.VMEM((4, TB, 512), bf16),
            pltpu.VMEM((8, TB, 256), bf16),
            pltpu.VMEM((8, TB, 256), bf16),
            pltpu.VMEM((8, 1, TB), jnp.int32),
            pltpu.VMEM((2, 4 * HB, 8 * TB), f32),
            pltpu.VMEM((4, 2, 4, 4 * HB, 128), bf16),
            pltpu.VMEM((32, CB), bf16),
            pltpu.VMEM((2, 2, 2, NZ, 16, CP), bf16),
            pltpu.VMEM((2, NZ, 64, CP), bf16),
            pltpu.VMEM((2, 4, HB, CP), bf16),
            pltpu.VMEM((2, 4, HB, CP), bf16),
            pltpu.VMEM((TB, D), bf16),
            pltpu.VMEM((1, D), f32),
            pltpu.VMEM((TB, D), bf16),
            dma((10,)),
            dma((4,)), dma((4,)),
            dma((8,)), dma((8,)),
            dma((8,)), dma((8,)),
            dma((8,)), dma((8,)),
            dma((NZ,)), dma((NZ,)),
            dma((4, 4)), dma((4, 4)),
            dma((5, 4)), dma((5, 4)),
            dma((2, 8)), dma((2, 8)),
            dma((2, 8)), dma((2, 8)),
            dma((2, 4)), dma((2, 4)),
        ],
        compiler_params=pltpu.CompilerParams(
            collective_id=0, has_side_effects=True, vmem_limit_bytes=60 << 20
        ),
    )(hidden_rows, query_proj, key_proj, value_proj, order_pos, post_gain, out_weight)


def solution(mesh):
    placed = (
        P("fsdp", "ctx", None),
        P("fsdp", "ctx", None),
        P("fsdp", "ctx", None),
        P("fsdp", "ctx", None),
        P("fsdp", "ctx"),
        P(),
        P("fsdp", "ctx"),
    )
    return jax.shard_map(
        shards, mesh=mesh, in_specs=placed, out_specs=P("fsdp", "ctx", None), check_vma=False
    )
```

```python
import jax
import jax.numpy as jnp
from jax import lax
from jax.experimental import pallas as pl
from jax.experimental.pallas import tpu as pltpu
from jax.sharding import PartitionSpec as P

D = 4608
TB = 128
HB = 64
CB = 576
CP = 2 * CB
NC = CP // 3
NZ = 16
INNER = 1.0 / 600.0
OUTER = 50.0 * 1.4426950408889634
NORM_EPS = 1e-06
MESH = pl.DeviceIdType.MESH
AWAY = [0, 1, -1, 2, -2, 3, -3, 4, -4, 5, -5, 6, -6, 7, -7, 8]


def body(
    hid, q, k, v, pos, gain, w, out,
    qbuf, kbuf, vbuf, pbuf, bias, att, wst, wf, wg, obuf, rows, hbuf, gbuf, res,
    loc, q_s, q_r, k_s, k_r, v_s, v_r, p_s, p_r, wz_s, wz_r, wx_s, wx_r,
    sb_s, sb_r, a_s, a_r, f_s, f_r, o_s, o_r,
):
    ctx = lax.axis_index("ctx")
    fs = lax.axis_index("fsdp")
    xh, y = ctx // 4, ctx % 4
    xl, z, core = fs // 32, (fs // 2) % NZ, fs % 2
    sends = []

    def dev_y(d):
        return (xh * 4 + (y + d) % 4, fs)

    def dev_ctx(flip, d):
        return (((xh + flip) % 2) * 4 + (y + d) % 4, fs)

    def at_x(d):
        return (xh * 2 + xl + d + 4) % 4

    def dev_x(d):
        return ((at_x(d) // 2) * 4 + y, (at_x(d) % 2) * 32 + fs % 32)

    x_opp = dev_ctx(1, 0)
    sibling = (ctx, fs + 1 - 2 * core)

    def dev_z(d):
        return (ctx, xl * 32 + ((z + d + NZ) % NZ) * 2 + core)

    def remote(src, dst, ss, rs, dev):
        return pltpu.make_async_remote_copy(
            src_ref=src, dst_ref=dst, send_sem=ss, recv_sem=rs, device_id=dev, device_id_type=MESH
        )

    def send(src, dst, ss, rs, dev):
        c = remote(src, dst, ss, rs, dev)
        c.start()
        sends.append(c)

    def arrived(dst, sem):
        remote(dst, dst, loc.at[6], sem, sibling).wait_recv()

    partners = [dev_ctx(f, d) for f in range(2) for d in range(4) if f or d]
    partners += [dev_x(1), dev_x(-1), sibling] + [dev_z(d) for d in AWAY[1:]]
    barrier = pltpu.get_barrier_semaphore()
    for dev in partners:
        pl.semaphore_signal(barrier, inc=1, device_id=dev, device_id_type=MESH)

    kcol = pl.multiple_of(y * 256, 256)
    qcol = pl.multiple_of(y * 512, 512)
    own = [
        pltpu.make_async_copy(w, wst, loc.at[0]),
        pltpu.make_async_copy(k.at[0, :, pl.ds(kcol, 256)], kbuf.at[ctx], loc.at[1]),
        pltpu.make_async_copy(v.at[0, :, pl.ds(kcol, 256)], vbuf.at[ctx], loc.at[2]),
        pltpu.make_async_copy(q.at[0, :, pl.ds(qcol, 512)], qbuf.at[y], loc.at[3]),
        pltpu.make_async_copy(pos, pbuf.at[ctx], loc.at[4]),
        pltpu.make_async_copy(hid.at[0], hbuf, loc.at[5]),
        pltpu.make_async_copy(gain, gbuf.at[0], loc.at[7]),
    ]
    for c in own:
        c.start()
    own[0].wait()
    wf[xh, xl, core, 0] = jnp.concatenate([wst[0:16], wst[16:32]], axis=1)
    pl.semaphore_wait(barrier, len(partners))

    for d in (1, 3, 2):
        col = pl.multiple_of(((y + d) % 4) * 256, 256)
        send(k.at[0, :, pl.ds(col, 256)], kbuf.at[ctx], k_s.at[d], k_r.at[d], dev_y(d))
        send(v.at[0, :, pl.ds(col, 256)], vbuf.at[ctx], v_s.at[d], v_r.at[d], dev_y(d))
    send(k.at[0, :, pl.ds(kcol, 256)], kbuf.at[ctx], k_s.at[4], k_r.at[4], x_opp)
    send(v.at[0, :, pl.ds(kcol, 256)], vbuf.at[ctx], v_s.at[4], v_r.at[4], x_opp)
    for f in range(2):
        for d in range(4):
            if f or d:
                i = f * 4 + d
                send(pos, pbuf.at[ctx], p_s.at[i], p_r.at[i], dev_ctx(f, d))

    def away(d):
        return AWAY.index(d if d < 8 else 8) if d > -8 else AWAY.index(8)

    own_w = wf.at[xh, xl, core, 0]
    for d in (1, -1, 4, -4, 2, -2, 3, -3):
        send(own_w, wf.at[xh, xl, core, away(-d)], wz_s.at[away(d)], wz_r.at[away(-d)], dev_z(d))
    for d in (1, 3, 2):
        col = pl.multiple_of(((y + d) % 4) * 512, 512)
        send(q.at[0, :, pl.ds(col, 512)], qbuf.at[y], q_s.at[d], q_r.at[d], dev_y(d))

    def forward_kv(d):
        src = xh * 4 + (y - d + 4) % 4
        arrived(kbuf.at[src], k_r.at[d])
        send(kbuf.at[src], kbuf.at[src], k_s.at[4 + d], k_r.at[4 + d], x_opp)
        arrived(vbuf.at[src], v_r.at[d])
        send(vbuf.at[src], vbuf.at[src], v_s.at[4 + d], v_r.at[4 + d], x_opp)

    forward_kv(1)
    forward_kv(3)
    for side in (1, -1):
        blk = wf.at[xh, xl, core, away(-4 * side)]
        arrived(blk, wz_r.at[away(-4 * side)])
        for e in (4, 3, 2, 1) if side > 0 else (3, 2, 1):
            r = away(-(4 + e) * side)
            send(blk, wf.at[xh, xl, core, r], wz_s.at[away((4 + e) * side)], wz_r.at[r], dev_z(e * side))
    forward_kv(2)

    def blocks(d, c, first, n):
        return wf.at[at_x(d) // 2, at_x(d) % 2, c, pl.ds(first, n)]

    def weights_z(b):
        for r in range(max(4 * b, 1), 4 * b + 4):
            if AWAY[r] not in (4, -4):
                arrived(wf.at[xh, xl, core, r], wz_r.at[r])
        src = blocks(0, core, 4 * b, 4)
        for side, d in enumerate((1, -1)):
            send(src, src, wx_s.at[side, b], wx_r.at[side, b], dev_x(d))
        send(src, src, sb_s.at[0, b], sb_r.at[0, b], sibling)

    def weights_x(b):
        for side, d in enumerate((1, -1)):
            src = blocks(-d, core, 4 * b, 4)
            arrived(src, wx_r.at[side, b])
            half = blocks(-d, core, 4 * b + 2 * side, 2)
            send(half, half, wx_s.at[2 + side, b], wx_r.at[2 + side, b], dev_x(d))
            send(src, src, sb_s.at[1 + side, b], sb_r.at[1 + side, b], sibling)

    def weights_far(b):
        for side in range(2):
            half = blocks(2, core, 4 * b + 2 * side, 2)
            arrived(half, wx_r.at[2 + side, b])
            send(half, half, sb_s.at[3 + side, b], sb_r.at[3 + side, b], sibling)

    def unfold(b):
        for i, d in enumerate((0, -1, 1)):
            arrived(blocks(d, 1 - core, 4 * b, 4), sb_r.at[i, b])
        for side in range(2):
            arrived(blocks(2, 1 - core, 4 * b + 2 * side, 2), sb_r.at[3 + side, b])

        def piece(i, _):
            l, c = i // 2, i % 2
            for r in range(4 * b, 4 * b + 4):
                zb = (z + AWAY[r] + NZ) % NZ
                lo, hi = wf[0, l, c, r], wf[1, l, c, r]
                top = pl.multiple_of(c * 32, 32)
                wg[l, zb, pl.ds(top, 16)] = jnp.concatenate([lo[:, :CB], hi[:, :CB]], axis=1)
                wg[l, zb, pl.ds(top + 16, 16)] = jnp.concatenate([lo[:, CB:], hi[:, CB:]], axis=1)
            return 0

        lax.fori_loop(0, 4, piece, 0)

    for f in range(2):
        for d in range(4):
            if f or d:
                arrived(pbuf.at[((xh + f) % 2) * 4 + (y - d + 4) % 4], p_r.at[f * 4 + d])
    own[4].wait()
    for t in range(4):
        prow = pbuf[xh * 4 + t].astype(jnp.float32)
        pcol = jnp.transpose(jnp.broadcast_to(prow, (TB, TB)), (1, 0))
        for c in range(8):
            seen = jnp.where(pbuf[c].astype(jnp.float32) <= pcol, 0.0, -1e30)
            for p in range(2):
                bias[p, t * HB : (t + 1) * HB, c * TB : (c + 1) * TB] = seen[p * HB : (p + 1) * HB]

    weights_z(0)
    for c in own[1:4] + own[5:]:
        c.wait()
    for d in (1, 3, 2):
        arrived(qbuf.at[(y - d + 4) % 4], q_r.at[d])
    weights_z(1)
    for d in range(4):
        src = (1 - xh) * 4 + (y - d + 4) % 4
        arrived(kbuf.at[src], k_r.at[4 + d])
        arrived(vbuf.at[src], v_r.at[4 + d])

    def attend(p, h):
        gcol = pl.multiple_of((h // 2) * 128, 128)
        qh = qbuf[:, pl.ds(pl.multiple_of(p * HB, HB), HB), pl.ds(pl.multiple_of(h * 128, 128), 128)]
        qh = qh.reshape(4 * HB, 128)
        num = den = 0.0
        for c in range(4):
            keys = kbuf[2 * c : 2 * c + 2, :, pl.ds(gcol, 128)].reshape(2 * TB, 128)
            vals = vbuf[2 * c : 2 * c + 2, :, pl.ds(gcol, 128)].reshape(2 * TB, 128)
            s = lax.dot_general(qh, keys, (((1,), (1,)), ((), ())), preferred_element_type=jnp.float32)
            e = jnp.exp2(jnp.tanh(s * INNER) * OUTER + bias[p, :, c * 256 : (c + 1) * 256])
            den += e[:, :128] + e[:, 128:]
            num += jnp.dot(e.astype(jnp.bfloat16), vals, preferred_element_type=jnp.float32)
        den = jnp.sum(den, axis=-1, keepdims=True)
        att[y, p, h] = (num / den).astype(jnp.bfloat16)

    def att_forward(u):
        p, h = u // 4, u % 4
        for side, d in enumerate((1, 3)):
            src = (y - d + 4) % 4
            arrived(att.at[src, p, h], a_r.at[side, u])
            half = att.at[src, p, h, pl.ds(side * TB, TB)]
            remote(half, half, f_s.at[side, u], f_r.at[side, u], dev_y(d)).start()

    def unit(u, _):
        p, h = u // 4, u % 4
        attend(p, h)
        blk = att.at[y, p, h]
        for side, d in enumerate((1, 3)):
            remote(blk, blk, a_s.at[side, u], a_r.at[side, u], dev_y(d)).start()

        @pl.when(u >= 4)
        def _():
            att_forward(u - 4)

        return 0

    lax.fori_loop(0, 2, unit, 0)
    weights_x(0)
    lax.fori_loop(2, 4, unit, 0)
    weights_z(2)
    lax.fori_loop(4, 6, unit, 0)
    weights_x(1)
    weights_z(3)
    lax.fori_loop(6, 8, unit, 0)
    weights_far(0)
    weights_x(2)
    att_forward(4)
    weights_far(1)
    unfold(0)
    att_forward(5)
    weights_x(3)

    far = (y + 2) % 4

    def far_arrived(p):
        for h in range(4):
            for side in range(2):
                arrived(att.at[far, p, h, pl.ds(side * TB, TB)], f_r.at[side, p * 4 + h])

    def project(p):
        def cols(n, _):
            col = pl.multiple_of(n * NC, NC)
            r = 0.0
            for src in range(4):
                a = jnp.concatenate([att[src, p, h] for h in range(4)], axis=1)
                wb = wg[src // 2, (src % 2) * 8 : (src % 2) * 8 + 8, :, pl.ds(col, NC)].reshape(512, NC)
                r += jnp.dot(a, wb, preferred_element_type=jnp.float32)
            obuf[p, n] = r.astype(jnp.bfloat16).reshape(4, HB, NC)
            for d in (2, 1, 3):
                remote(
                    obuf.at[p, n, (y + d) % 4], rows.at[p, n, y], o_s.at[p, n, d], o_r.at[p, n, d], dev_y(d)
                ).start()
            rows[p, n, y] = obuf[p, n, y]
            return 0

        lax.fori_loop(0, 3, cols, 0)

    def norm(p):
        for d in (1, 3, 2):
            for n in range(3):
                arrived(rows.at[p, n, (y - d + 4) % 4], o_r.at[p, n, d])

        def piece(i, _):
            r = pl.ds(pl.multiple_of(i * 32, 32), 32)
            t = pl.ds(pl.multiple_of(p * HB + i * 32, 32), 32)
            ss = jnp.zeros((32, 1), jnp.float32)
            for c in range(4):
                x = jnp.concatenate([rows[p, n, c, r] for n in range(3)], axis=1).astype(jnp.float32)
                ss += jnp.sum(x * x, axis=-1, keepdims=True)
            scale = lax.rsqrt(ss * (1.0 / D) + NORM_EPS)
            for c in range(4):
                x = jnp.concatenate([rows[p, n, c, r] for n in range(3)], axis=1).astype(jnp.float32) * scale
                for b in range(2):
                    cols = slice(b * 4 * CB + c * CB, b * 4 * CB + (c + 1) * CB)
                    scaled = x[:, b * CB : (b + 1) * CB] * gbuf[:, cols]
                    res[t, cols] = (hbuf[t, cols].astype(jnp.float32) + scaled).astype(jnp.bfloat16)
            return 0

        lax.fori_loop(0, 2, piece, 0)
        done = pl.ds(p * HB, HB)
        return pltpu.make_async_copy(res.at[done], out.at[0, done], loc.at[8 + p])

    weights_far(2)
    unfold(1)
    att_forward(6)
    weights_far(3)
    unfold(2)
    att_forward(7)
    far_arrived(0)
    unfold(3)
    project(0)
    far_arrived(1)
    project(1)
    first = norm(0)
    first.start()
    second = norm(1)
    second.start()
    first.wait()
    second.wait()

    for c in sends:
        c.wait_send()
    for p in range(2):
        for n in range(3):
            for d in (1, 2, 3):
                remote(obuf.at[p, n, 0], obuf.at[p, n, 0], o_s.at[p, n, d], loc.at[6], sibling).wait_send()
    for u in range(8):
        for side in range(2):
            blk = att.at[0, 0, 0]
            remote(blk, blk, a_s.at[side, u], loc.at[6], sibling).wait_send()
            blk = att.at[0, 0, 0, pl.ds(0, TB)]
            remote(blk, blk, f_s.at[side, u], loc.at[6], sibling).wait_send()


def shards(hidden_rows, query_proj, key_proj, value_proj, order_pos, post_gain, out_weight):
    hbm = pl.BlockSpec(memory_space=pl.ANY)
    bf16, f32, dma = jnp.bfloat16, jnp.float32, pltpu.SemaphoreType.DMA
    return pl.pallas_call(
        body,
        name="sublayer",
        out_shape=jax.ShapeDtypeStruct((1, TB, D), bf16),
        in_specs=[hbm] * 7,
        out_specs=hbm,
        scratch_shapes=[
            pltpu.VMEM((4, TB, 512), bf16),
            pltpu.VMEM((8, TB, 256), bf16),
            pltpu.VMEM((8, TB, 256), bf16),
            pltpu.VMEM((8, 1, TB), jnp.int32),
            pltpu.VMEM((2, 4 * HB, 8 * TB), f32),
            pltpu.VMEM((4, 2, 4, 4 * HB, 128), bf16),
            pltpu.VMEM((32, CB), bf16),
            pltpu.VMEM((2, 2, 2, NZ, 16, CP), bf16),
            pltpu.VMEM((2, NZ, 64, CP), bf16),
            pltpu.VMEM((2, 3, 4, HB, NC), bf16),
            pltpu.VMEM((2, 3, 4, HB, NC), bf16),
            pltpu.VMEM((TB, D), bf16),
            pltpu.VMEM((1, D), f32),
            pltpu.VMEM((TB, D), bf16),
            dma((10,)),
            dma((4,)), dma((4,)),
            dma((8,)), dma((8,)),
            dma((8,)), dma((8,)),
            dma((8,)), dma((8,)),
            dma((NZ,)), dma((NZ,)),
            dma((4, 4)), dma((4, 4)),
            dma((5, 4)), dma((5, 4)),
            dma((2, 8)), dma((2, 8)),
            dma((2, 8)), dma((2, 8)),
            dma((2, 3, 4)), dma((2, 3, 4)),
        ],
        compiler_params=pltpu.CompilerParams(
            collective_id=0, has_side_effects=True, vmem_limit_bytes=60 << 20
        ),
    )(hidden_rows, query_proj, key_proj, value_proj, order_pos, post_gain, out_weight)


def solution(mesh):
    placed = (
        P("fsdp", "ctx", None),
        P("fsdp", "ctx", None),
        P("fsdp", "ctx", None),
        P("fsdp", "ctx", None),
        P("fsdp", "ctx"),
        P(),
        P("fsdp", "ctx"),
    )
    return jax.shard_map(
        shards, mesh=mesh, in_specs=placed, out_specs=P("fsdp", "ctx", None), check_vma=False
    )
```

```python
import jax
import jax.numpy as jnp
from jax import lax
from jax.experimental import pallas as pl
from jax.experimental.pallas import tpu as pltpu
from jax.sharding import PartitionSpec as P

D = 4608
TB = 128
HB = 64
CB = 576
CP = 2 * CB
NC = CP // 3
NZ = 16
INNER = 1.0 / 600.0
OUTER = 50.0 * 1.4426950408889634
NORM_EPS = 1e-06
MESH = pl.DeviceIdType.MESH
AWAY = [0, 1, -1, 2, -2, 3, -3, 4, -4, 5, -5, 6, -6, 7, -7, 8]


def body(
    hid, q, k, v, pos, gain, w, out,
    qbuf, kbuf, vbuf, pbuf, bias, att, wst, wf, wg, obuf, rows, hbuf, gbuf, res,
    loc, q_s, q_r, k_s, k_r, v_s, v_r, p_s, p_r, wz_s, wz_r, wx_s, wx_r,
    sb_s, sb_r, a_s, a_r, f_s, f_r, o_s, o_r,
):
    ctx = lax.axis_index("ctx")
    fs = lax.axis_index("fsdp")
    xh, y = ctx // 4, ctx % 4
    xl, z, core = fs // 32, (fs // 2) % NZ, fs % 2
    sends = []

    def dev_y(d):
        return (xh * 4 + (y + d) % 4, fs)

    def dev_ctx(flip, d):
        return (((xh + flip) % 2) * 4 + (y + d) % 4, fs)

    def at_x(d):
        return (xh * 2 + xl + d + 4) % 4

    def dev_x(d):
        return ((at_x(d) // 2) * 4 + y, (at_x(d) % 2) * 32 + fs % 32)

    x_opp = dev_ctx(1, 0)
    sibling = (ctx, fs + 1 - 2 * core)

    def dev_z(d):
        return (ctx, xl * 32 + ((z + d + NZ) % NZ) * 2 + core)

    def remote(src, dst, ss, rs, dev):
        return pltpu.make_async_remote_copy(
            src_ref=src, dst_ref=dst, send_sem=ss, recv_sem=rs, device_id=dev, device_id_type=MESH
        )

    def send(src, dst, ss, rs, dev):
        c = remote(src, dst, ss, rs, dev)
        c.start()
        sends.append(c)

    def arrived(dst, sem):
        remote(dst, dst, loc.at[6], sem, sibling).wait_recv()

    partners = [dev_ctx(f, d) for f in range(2) for d in range(4) if f or d]
    partners += [dev_x(1), dev_x(-1), sibling] + [dev_z(d) for d in AWAY[1:]]
    barrier = pltpu.get_barrier_semaphore()
    for dev in partners:
        pl.semaphore_signal(barrier, inc=1, device_id=dev, device_id_type=MESH)

    kcol = pl.multiple_of(y * 256, 256)
    qcol = pl.multiple_of(y * 512, 512)
    own = [
        pltpu.make_async_copy(w, wst, loc.at[0]),
        pltpu.make_async_copy(k.at[0, :, pl.ds(kcol, 256)], kbuf.at[ctx], loc.at[1]),
        pltpu.make_async_copy(v.at[0, :, pl.ds(kcol, 256)], vbuf.at[ctx], loc.at[2]),
        pltpu.make_async_copy(q.at[0, :, pl.ds(qcol, 512)], qbuf.at[y], loc.at[3]),
        pltpu.make_async_copy(pos, pbuf.at[ctx], loc.at[4]),
        pltpu.make_async_copy(hid.at[0], hbuf, loc.at[5]),
        pltpu.make_async_copy(gain, gbuf.at[0], loc.at[7]),
    ]
    for c in own:
        c.start()
    own[0].wait()
    wf[xh, xl, core, 0] = jnp.concatenate([wst[0:16], wst[16:32]], axis=1)
    pl.semaphore_wait(barrier, len(partners))

    for d in (1, 3, 2):
        col = pl.multiple_of(((y + d) % 4) * 256, 256)
        send(k.at[0, :, pl.ds(col, 256)], kbuf.at[ctx], k_s.at[d], k_r.at[d], dev_y(d))
        send(v.at[0, :, pl.ds(col, 256)], vbuf.at[ctx], v_s.at[d], v_r.at[d], dev_y(d))
    send(k.at[0, :, pl.ds(kcol, 256)], kbuf.at[ctx], k_s.at[4], k_r.at[4], x_opp)
    send(v.at[0, :, pl.ds(kcol, 256)], vbuf.at[ctx], v_s.at[4], v_r.at[4], x_opp)
    for f in range(2):
        for d in range(4):
            if f or d:
                i = f * 4 + d
                send(pos, pbuf.at[ctx], p_s.at[i], p_r.at[i], dev_ctx(f, d))

    def away(d):
        return AWAY.index(d if d < 8 else 8) if d > -8 else AWAY.index(8)

    own_w = wf.at[xh, xl, core, 0]
    for d in (1, -1, 4, -4, 2, -2, 3, -3):
        send(own_w, wf.at[xh, xl, core, away(-d)], wz_s.at[away(d)], wz_r.at[away(-d)], dev_z(d))
    for d in (1, 3, 2):
        col = pl.multiple_of(((y + d) % 4) * 512, 512)
        send(q.at[0, :, pl.ds(col, 512)], qbuf.at[y], q_s.at[d], q_r.at[d], dev_y(d))

    def forward_kv(d):
        src = xh * 4 + (y - d + 4) % 4
        arrived(kbuf.at[src], k_r.at[d])
        send(kbuf.at[src], kbuf.at[src], k_s.at[4 + d], k_r.at[4 + d], x_opp)
        arrived(vbuf.at[src], v_r.at[d])
        send(vbuf.at[src], vbuf.at[src], v_s.at[4 + d], v_r.at[4 + d], x_opp)

    forward_kv(1)
    forward_kv(3)
    forward_kv(2)
    for side in (1, -1):
        blk = wf.at[xh, xl, core, away(-4 * side)]
        arrived(blk, wz_r.at[away(-4 * side)])
        for e in (4, 3, 2, 1) if side > 0 else (3, 2, 1):
            r = away(-(4 + e) * side)
            send(blk, wf.at[xh, xl, core, r], wz_s.at[away((4 + e) * side)], wz_r.at[r], dev_z(e * side))

    def blocks(d, c, first, n):
        return wf.at[at_x(d) // 2, at_x(d) % 2, c, pl.ds(first, n)]

    def weights_z(b):
        for r in range(max(4 * b, 1), 4 * b + 4):
            if AWAY[r] not in (4, -4):
                arrived(wf.at[xh, xl, core, r], wz_r.at[r])
        src = blocks(0, core, 4 * b, 4)
        for side, d in enumerate((1, -1)):
            send(src, src, wx_s.at[side, b], wx_r.at[side, b], dev_x(d))
        send(src, src, sb_s.at[0, b], sb_r.at[0, b], sibling)

    def weights_x(b):
        for side, d in enumerate((1, -1)):
            src = blocks(-d, core, 4 * b, 4)
            arrived(src, wx_r.at[side, b])
            half = blocks(-d, core, 4 * b + 2 * side, 2)
            send(half, half, wx_s.at[2 + side, b], wx_r.at[2 + side, b], dev_x(d))
            send(src, src, sb_s.at[1 + side, b], sb_r.at[1 + side, b], sibling)

    def weights_far(b):
        for side in range(2):
            half = blocks(2, core, 4 * b + 2 * side, 2)
            arrived(half, wx_r.at[2 + side, b])
            send(half, half, sb_s.at[3 + side, b], sb_r.at[3 + side, b], sibling)

    def unfold(b):
        for i, d in enumerate((0, -1, 1)):
            arrived(blocks(d, 1 - core, 4 * b, 4), sb_r.at[i, b])
        for side in range(2):
            arrived(blocks(2, 1 - core, 4 * b + 2 * side, 2), sb_r.at[3 + side, b])

        def piece(i, _):
            l, c = i // 2, i % 2
            for r in range(4 * b, 4 * b + 4):
                zb = (z + AWAY[r] + NZ) % NZ
                lo, hi = wf[0, l, c, r], wf[1, l, c, r]
                top = pl.multiple_of(c * 32, 32)
                wg[l, zb, pl.ds(top, 16)] = jnp.concatenate([lo[:, :CB], hi[:, :CB]], axis=1)
                wg[l, zb, pl.ds(top + 16, 16)] = jnp.concatenate([lo[:, CB:], hi[:, CB:]], axis=1)
            return 0

        lax.fori_loop(0, 4, piece, 0)

    for f in range(2):
        for d in range(4):
            if f or d:
                arrived(pbuf.at[((xh + f) % 2) * 4 + (y - d + 4) % 4], p_r.at[f * 4 + d])
    own[4].wait()
    for t in range(4):
        prow = pbuf[xh * 4 + t].astype(jnp.float32)
        pcol = jnp.transpose(jnp.broadcast_to(prow, (TB, TB)), (1, 0))
        for c in range(8):
            seen = jnp.where(pbuf[c].astype(jnp.float32) <= pcol, 0.0, -1e30)
            for p in range(2):
                bias[p, t * HB : (t + 1) * HB, c * TB : (c + 1) * TB] = seen[p * HB : (p + 1) * HB]

    weights_z(0)
    for c in own[1:4] + own[5:]:
        c.wait()
    for d in (1, 3, 2):
        arrived(qbuf.at[(y - d + 4) % 4], q_r.at[d])
    weights_z(1)
    for d in range(4):
        src = (1 - xh) * 4 + (y - d + 4) % 4
        arrived(kbuf.at[src], k_r.at[4 + d])
        arrived(vbuf.at[src], v_r.at[4 + d])

    def attend(p, h):
        gcol = pl.multiple_of((h // 2) * 128, 128)
        qh = qbuf[:, pl.ds(pl.multiple_of(p * HB, HB), HB), pl.ds(pl.multiple_of(h * 128, 128), 128)]
        qh = qh.reshape(4 * HB, 128)
        num = den = 0.0
        for c in range(4):
            keys = kbuf[2 * c : 2 * c + 2, :, pl.ds(gcol, 128)].reshape(2 * TB, 128)
            vals = vbuf[2 * c : 2 * c + 2, :, pl.ds(gcol, 128)].reshape(2 * TB, 128)
            s = lax.dot_general(qh, keys, (((1,), (1,)), ((), ())), preferred_element_type=jnp.float32)
            e = jnp.exp2(jnp.tanh(s * INNER) * OUTER + bias[p, :, c * 256 : (c + 1) * 256])
            den += e[:, :128] + e[:, 128:]
            num += jnp.dot(e.astype(jnp.bfloat16), vals, preferred_element_type=jnp.float32)
        den = jnp.sum(den, axis=-1, keepdims=True)
        att[y, p, h] = (num / den).astype(jnp.bfloat16)

    def att_forward(u):
        p, h = u // 4, u % 4
        for side, d in enumerate((1, 3)):
            src = (y - d + 4) % 4
            arrived(att.at[src, p, h], a_r.at[side, u])
            half = att.at[src, p, h, pl.ds(side * TB, TB)]
            remote(half, half, f_s.at[side, u], f_r.at[side, u], dev_y(d)).start()

    def unit(u, _):
        p, h = u // 4, u % 4
        attend(p, h)
        blk = att.at[y, p, h]
        for side, d in enumerate((1, 3)):
            remote(blk, blk, a_s.at[side, u], a_r.at[side, u], dev_y(d)).start()

        @pl.when(u >= 4)
        def _():
            att_forward(u - 4)

        return 0

    lax.fori_loop(0, 2, unit, 0)
    weights_x(0)
    lax.fori_loop(2, 4, unit, 0)
    weights_z(2)
    lax.fori_loop(4, 6, unit, 0)
    weights_x(1)
    weights_z(3)
    lax.fori_loop(6, 8, unit, 0)
    weights_far(0)
    weights_x(2)
    att_forward(4)
    weights_far(1)
    unfold(0)
    att_forward(5)
    weights_x(3)

    far = (y + 2) % 4

    def far_arrived(p):
        for h in range(4):
            for side in range(2):
                arrived(att.at[far, p, h, pl.ds(side * TB, TB)], f_r.at[side, p * 4 + h])

    def project(p):
        def cols(n, _):
            col = pl.multiple_of(n * NC, NC)
            r = 0.0
            for src in range(4):
                a = jnp.concatenate([att[src, p, h] for h in range(4)], axis=1)
                wb = wg[src // 2, (src % 2) * 8 : (src % 2) * 8 + 8, :, pl.ds(col, NC)].reshape(512, NC)
                r += jnp.dot(a, wb, preferred_element_type=jnp.float32)
            obuf[p, n] = r.astype(jnp.bfloat16).reshape(4, HB, NC)
            for d in (2, 1, 3):
                remote(
                    obuf.at[p, n, (y + d) % 4], rows.at[p, n, y], o_s.at[p, n, d], o_r.at[p, n, d], dev_y(d)
                ).start()
            rows[p, n, y] = obuf[p, n, y]
            return 0

        lax.fori_loop(0, 3, cols, 0)

    def norm(p):
        for d in (1, 3, 2):
            for n in range(3):
                arrived(rows.at[p, n, (y - d + 4) % 4], o_r.at[p, n, d])

        def piece(i, _):
            r = pl.ds(pl.multiple_of(i * 32, 32), 32)
            t = pl.ds(pl.multiple_of(p * HB + i * 32, 32), 32)
            ss = jnp.zeros((32, 1), jnp.float32)
            for c in range(4):
                x = jnp.concatenate([rows[p, n, c, r] for n in range(3)], axis=1).astype(jnp.float32)
                ss += jnp.sum(x * x, axis=-1, keepdims=True)
            scale = lax.rsqrt(ss * (1.0 / D) + NORM_EPS)
            for c in range(4):
                x = jnp.concatenate([rows[p, n, c, r] for n in range(3)], axis=1).astype(jnp.float32) * scale
                for b in range(2):
                    cols = slice(b * 4 * CB + c * CB, b * 4 * CB + (c + 1) * CB)
                    scaled = x[:, b * CB : (b + 1) * CB] * gbuf[:, cols]
                    res[t, cols] = (hbuf[t, cols].astype(jnp.float32) + scaled).astype(jnp.bfloat16)
            return 0

        lax.fori_loop(0, 2, piece, 0)
        done = pl.ds(p * HB, HB)
        return pltpu.make_async_copy(res.at[done], out.at[0, done], loc.at[8 + p])

    weights_far(2)
    unfold(1)
    att_forward(6)
    weights_far(3)
    unfold(2)
    att_forward(7)
    far_arrived(0)
    unfold(3)
    project(0)
    far_arrived(1)
    project(1)
    first = norm(0)
    first.start()
    second = norm(1)
    second.start()
    first.wait()
    second.wait()

    for c in sends:
        c.wait_send()
    for p in range(2):
        for n in range(3):
            for d in (1, 2, 3):
                remote(obuf.at[p, n, 0], obuf.at[p, n, 0], o_s.at[p, n, d], loc.at[6], sibling).wait_send()
    for u in range(8):
        for side in range(2):
            blk = att.at[0, 0, 0]
            remote(blk, blk, a_s.at[side, u], loc.at[6], sibling).wait_send()
            blk = att.at[0, 0, 0, pl.ds(0, TB)]
            remote(blk, blk, f_s.at[side, u], loc.at[6], sibling).wait_send()


def shards(hidden_rows, query_proj, key_proj, value_proj, order_pos, post_gain, out_weight):
    hbm = pl.BlockSpec(memory_space=pl.ANY)
    bf16, f32, dma = jnp.bfloat16, jnp.float32, pltpu.SemaphoreType.DMA
    return pl.pallas_call(
        body,
        name="sublayer",
        out_shape=jax.ShapeDtypeStruct((1, TB, D), bf16),
        in_specs=[hbm] * 7,
        out_specs=hbm,
        scratch_shapes=[
            pltpu.VMEM((4, TB, 512), bf16),
            pltpu.VMEM((8, TB, 256), bf16),
            pltpu.VMEM((8, TB, 256), bf16),
            pltpu.VMEM((8, 1, TB), jnp.int32),
            pltpu.VMEM((2, 4 * HB, 8 * TB), f32),
            pltpu.VMEM((4, 2, 4, 4 * HB, 128), bf16),
            pltpu.VMEM((32, CB), bf16),
            pltpu.VMEM((2, 2, 2, NZ, 16, CP), bf16),
            pltpu.VMEM((2, NZ, 64, CP), bf16),
            pltpu.VMEM((2, 3, 4, HB, NC), bf16),
            pltpu.VMEM((2, 3, 4, HB, NC), bf16),
            pltpu.VMEM((TB, D), bf16),
            pltpu.VMEM((1, D), f32),
            pltpu.VMEM((TB, D), bf16),
            dma((10,)),
            dma((4,)), dma((4,)),
            dma((8,)), dma((8,)),
            dma((8,)), dma((8,)),
            dma((8,)), dma((8,)),
            dma((NZ,)), dma((NZ,)),
            dma((4, 4)), dma((4, 4)),
            dma((5, 4)), dma((5, 4)),
            dma((2, 8)), dma((2, 8)),
            dma((2, 8)), dma((2, 8)),
            dma((2, 3, 4)), dma((2, 3, 4)),
        ],
        compiler_params=pltpu.CompilerParams(
            collective_id=0, has_side_effects=True, vmem_limit_bytes=60 << 20
        ),
    )(hidden_rows, query_proj, key_proj, value_proj, order_pos, post_gain, out_weight)


def solution(mesh):
    placed = (
        P("fsdp", "ctx", None),
        P("fsdp", "ctx", None),
        P("fsdp", "ctx", None),
        P("fsdp", "ctx", None),
        P("fsdp", "ctx"),
        P(),
        P("fsdp", "ctx"),
    )
    return jax.shard_map(
        shards, mesh=mesh, in_specs=placed, out_specs=P("fsdp", "ctx", None), check_vma=False
    )
```
